256 devices in a mesh: seq: 8 (over x, core), exp: 32 (over y, z).
Axes of the slice: x: 4, y: 4, z: 8, core: 2. Of those that a mesh axis runs over, the one named last changes fastest.
Arguments:
- tokens: bfloat16 [4096, 7168], P('exp', 'seq'), may hold values from -6 to 6
- out_grad: bfloat16 [4096, 7168], P('exp', 'seq'), may hold values from -6 to 6
- expert_ids: int32 [4096, 8], P('exp'), may hold values from 0 to 255, as said below
- route_weights: float32 [4096, 8], P('exp'), may hold values from 0.2 to 2.5
- gate_proj: bfloat16 [32, 7168, 2048], P('exp', None, 'seq'), may hold values from -0.0625 to 0.0625
- up_proj: bfloat16 [32, 7168, 2048], P('exp', None, 'seq'), may hold values from -0.0625 to 0.0625
- down_proj: bfloat16 [32, 2048, 7168], P('exp', 'seq'), may hold values from -0.125 to 0.125
Outputs:
- token_grad: bfloat16 [4096, 7168], P('exp', 'seq')
- route_grad: float32 [4096, 8], P('exp', 'seq')
The draws below stay inside these ranges and needn't reach their ends.
Inputs may be any that keep to these rules, and one draw needn't show every extreme that they name: `expert_ids`: each row names 8 different experts, at most one of them below 32; between 96 and all of the 128 rows of one index of exp name one below 32; those rows name any one expert below 32 at most 8 times, and in every draw one such expert exactly 8 times on every index of exp.
All inputs are finite; a program needn't handle non-finite values.
Results may differ from the reference program's by a relative error of at most 0.0049.
Values may be sent and summed in bfloat16 or wider, within the bound.
A program may use at most 128 MiB of HBM per device.

```python
import math
import jax
import jax.numpy as jnp
from jax import lax

D = 7168
FF = 2048
TOPK = 8
TOK_DEV = 128
EXPERTS = 32
ROUTED = 256
MOST = 8
TOKENS = 4096
N_EXP = 32


def draw_expert_ids(key, part):
    block_count = TOKENS // TOK_DEV
    pool_size = EXPERTS * MOST
    outside_count = ROUTED - EXPERTS
    hottest = jax.random.randint(jax.random.fold_in(key, 1), (), 0, EXPERTS)
    favour = jax.random.randint(jax.random.fold_in(key, 2), (EXPERTS,), 1, 9)
    entries = jnp.arange(pool_size, dtype=jnp.int32)
    owners = entries // MOST

    def one_block(block_index):
        block_key = jax.random.fold_in(key, 1000 + block_index)
        subkeys = jax.random.split(block_key, 5)
        jitter = jax.random.randint(subkeys[0], (pool_size,), 0, 4096)
        scores = jnp.where(owners == hottest, 0, 1 + jitter // favour[owners])
        ranking = jnp.argsort(scores * pool_size + entries, stable=True)
        picked = owners[ranking][:TOK_DEV]
        live_rows = TOK_DEV - jax.random.randint(subkeys[1], (), 0, TOK_DEV // 4 + 1)
        window_ids = jnp.where(jnp.arange(TOK_DEV, dtype=jnp.int32) < live_rows, picked, -1)
        window_ids = window_ids[jax.random.permutation(subkeys[2], TOK_DEV)]
        offsets = jax.random.randint(subkeys[3], (TOK_DEV, 1), 0, outside_count)
        strides = jnp.arange(TOPK, dtype=jnp.int32)[None, :] * (outside_count // TOPK)
        outside_ids = EXPERTS + (offsets + strides) % outside_count
        position = jax.random.randint(subkeys[4], (TOK_DEV, 1), 0, TOPK)
        chosen = (jnp.arange(TOPK, dtype=jnp.int32)[None, :] == position) & (window_ids[:, None] >= 0)
        return jnp.where(chosen, window_ids[:, None], outside_ids)
    drawn = jax.vmap(one_block)(jnp.arange(block_count, dtype=jnp.int32))
    return drawn.reshape(TOKENS, TOPK).astype(jnp.int32)


def steps_of(stream_key, dims, cuts, least, top_value):
    level, own = 1.0, jax.random.fold_in(stream_key, 6)
    for axis_at, blocks in cuts:
        draws = jnp.exp(jax.random.uniform(jax.random.fold_in(own, axis_at), (blocks,), jnp.float32, least / len(cuts), top_value / len(cuts)))
        level = level * jnp.repeat(draws, dims[axis_at] // blocks).reshape([-1 if axis == axis_at else 1 for axis in range(len(dims))])
    return level


def bell_draw(key, dims, width, bound, shards=(), kind=jnp.bfloat16):
    values = width * jax.random.normal(key, dims, jnp.float32)
    if shards:
        values = values * steps_of(key, dims, shards, -0.22, 0.18)
    return jnp.clip(values, -bound, bound).astype(kind)


def setup_inputs(seed: int = 0) -> dict:
    streams_of = jax.random.split(jax.random.key(seed), 8)
    return {
        "tokens": bell_draw(streams_of[0], (TOKENS, D), 1.0, 6.0, ((0, 32), (1, 8))),
        "out_grad": bell_draw(streams_of[1], (TOKENS, D), 1.0, 6.0, ((0, 32), (1, 8))),
        "expert_ids": draw_expert_ids(jax.random.fold_in(streams_of[7], 71), 0),
        "route_weights": jnp.clip(jnp.exp(math.log(2.5) - 2.5257286 * jax.random.uniform(streams_of[3], (TOKENS, TOPK), jnp.float32) ** steps_of(streams_of[3], (TOKENS, TOPK), ((0, 32),), -0.2, 0.2)), 0.2, 2.5),
        "gate_proj": bell_draw(streams_of[4], (EXPERTS, D, FF), D ** -0.5, 0.0625, ((0, 32), (2, 8))),
        "up_proj": bell_draw(streams_of[5], (EXPERTS, D, FF), D ** -0.5, 0.0625, ((0, 32), (2, 8))),
        "down_proj": bell_draw(streams_of[6], (EXPERTS, FF, D), FF ** -0.5, 0.125, ((0, 32), (1, 8))),
    }


def expert_front(row_inputs, row_grads, w_gate, w_up, w_down):
    pre_gate = jnp.dot(row_inputs, w_gate, preferred_element_type=jnp.float32)
    pre_up = jnp.dot(row_inputs, w_up, preferred_element_type=jnp.float32)
    back_grad = jnp.dot(row_grads, w_down.T, preferred_element_type=jnp.float32)
    gate_sig = jax.nn.sigmoid(pre_gate)
    active = pre_gate * gate_sig
    route_part = jnp.sum(active * pre_up * back_grad, axis=-1)
    grad_gate = (back_grad * pre_up * gate_sig * (1.0 + pre_gate * (1.0 - gate_sig))).astype(jnp.bfloat16)
    grad_up = (back_grad * active).astype(jnp.bfloat16)
    return grad_gate, grad_up, route_part


def expert_back(grad_gate, grad_up, w_gate, w_up):
    return (jnp.dot(grad_gate, w_gate.T, preferred_element_type=jnp.float32)
            + jnp.dot(grad_up, w_up.T, preferred_element_type=jnp.float32))


def reference(tokens, out_grad, expert_ids, route_weights, gate_proj, up_proj, down_proj):
    capacity = N_EXP * MOST
    pair_count = TOKENS * TOPK
    flat_ids = expert_ids.reshape(-1)
    flat_weights = jnp.concatenate([route_weights.reshape(-1), jnp.zeros((1,), jnp.float32)])
    padded_x = jnp.concatenate([tokens, jnp.zeros((1, D), jnp.bfloat16)], axis=0)
    padded_dy = jnp.concatenate([out_grad, jnp.zeros((1, D), jnp.bfloat16)], axis=0)

    def visit_expert(running, expert):
        grad_total, route_total = running
        located = jnp.nonzero(flat_ids == expert, size=capacity, fill_value=pair_count)[0].astype(jnp.int32)
        token_row = (located // TOPK).astype(jnp.int32)
        w_gate = gate_proj[expert]
        w_up = up_proj[expert]
        grad_gate, grad_up, route_part = expert_front(padded_x[token_row], padded_dy[token_row], w_gate, w_up, down_proj[expert])
        pair_grad = expert_back(grad_gate, grad_up, w_gate, w_up)
        grad_total = grad_total.at[token_row].add(flat_weights[located][:, None] * pair_grad)
        route_total = route_total.at[located].add(route_part)
        return (grad_total, route_total), None

    initial = (jnp.zeros((TOKENS + 1, D), jnp.float32), jnp.zeros((pair_count + 1,), jnp.float32))
    (grad_total, route_total), _ = lax.scan(visit_expert, initial, jnp.arange(EXPERTS, dtype=jnp.int32))
    return grad_total[:TOKENS].astype(jnp.bfloat16), route_total[:pair_count].reshape(TOKENS, TOPK)
```

```python
import jax
import jax.numpy as jnp
from jax import lax
from jax.experimental import pallas as pl
from jax.experimental.pallas import tpu as pltpu
from jax.sharding import PartitionSpec as P

MESH = pl.DeviceIdType.MESH
BF = jnp.bfloat16
F32 = jnp.float32
NX, NC, NY, NZ = 4, 2, 4, 8
NE = NY * NZ
MOST = 8
SLOTS = NE * MOST
CHUNKS = 4
PER = NE // CHUNKS
NT = (((1,), (1,)), ((), ()))
TN = (((0,), (0,)), ((), ()))


def z_step(index):
    half = (index + 1) // 2
    return (NZ + half * (2 * (index % 2) - 1)) % NZ


def kernel(tok, og, ids, rw, wg_h, wu_h, wd_h, tg_out, rg_out,
           wgu, wd, packed, xg, acc, gbuf, ps, pb, own, relay, snd, fin, rets, ret,
           selbuf, rpart, rtot, rret,
           wsem, disp_r, ag_r, far_r, core_r, pair_r, rel_r, fin_r, ret_r, rp_r, rr_r, send_s):
    seq, exp = lax.axis_index("seq"), lax.axis_index("exp")
    x, c = seq // NC, seq % NC
    y, z = exp // NZ, exp % NZ
    f = tok.shape[1]

    def at_x(step, flip=0):
        return {"seq": NC * ((x + step) % NX) + (c + flip) % NC}

    def to_exp(j):
        dz = z_step(j // NY)
        return {"exp": ((y + j % NY) % NY) * NZ + (z + dz) % NZ}

    def from_exp(j):
        dz = z_step(j // NY)
        return {"exp": ((y + NY - j % NY) % NY) * NZ + (z + NZ - dz) % NZ}

    def copy(src, dst, ssem, rsem, dev):
        return pltpu.make_async_remote_copy(
            src_ref=src, dst_ref=dst, send_sem=ssem, recv_sem=rsem,
            device_id=dev, device_id_type=MESH)

    def got(ref, sem):
        pltpu.make_async_copy(ref, ref, sem).wait()

    wcopies = []
    for k in range(NX * NC):
        dx, flip = k // NC, k % NC
        first = pl.multiple_of((NC * ((x + NX - dx) % NX) + (c + flip) % NC) * f, 128)
        h = wg_h.shape[1]
        for n, (src, dst) in enumerate((
                (wg_h.at[pl.ds(first, f), :], wgu.at[k, :, 0:h]),
                (wu_h.at[pl.ds(first, f), :], wgu.at[k, :, h:2 * h]),
                (wd_h.at[:, pl.ds(first, f)], wd.at[k]))):
            one = pltpu.make_async_copy(src, dst, wsem.at[k, n])
            one.start()
            wcopies.append(one)

    barrier = pltpu.get_barrier_semaphore()

    @pl.loop(1, NE)
    def _(j):
        pl.semaphore_signal(barrier, inc=1, device_id=to_exp(j), device_id_type=MESH)

    for k in range(1, NX * NC):
        pl.semaphore_signal(barrier, inc=1, device_id=at_x(k // NC, k % NC), device_id_type=MESH)

    q = lax.broadcasted_iota(jnp.int32, (SLOTS, tok.shape[0]), 0)
    j = q >> 3
    i = j >> 2
    half = (i + 1) >> 1
    dz = (NZ + half * (2 * (i & 1) - 1)) & (NZ - 1)
    wanted = ((y + (j & 3)) & 3) * NZ + ((z + dz) & 7)
    hot = ids[0:1, :] == wanted
    for k in range(1, ids.shape[0]):
        hot = hot | (ids[k:k + 1, :] == wanted)
    hot = jnp.where(hot, 1.0, 0.0)
    t0 = lax.broadcasted_iota(jnp.int32, (tok.shape[0], tok.shape[0]), 0)
    t1 = lax.broadcasted_iota(jnp.int32, (tok.shape[0], tok.shape[0]), 1)
    before = jnp.where(t0 < t1, 1.0, 0.0).astype(BF)
    rank = jnp.dot(hot.astype(BF), before, preferred_element_type=F32)
    sel = jnp.where(rank == (q & 7).astype(F32), hot, 0.0)
    selbuf[...] = sel
    selb = sel.astype(BF)
    for n, src in enumerate((tok, og)):
        rows = jnp.dot(selb, src[...], preferred_element_type=F32)
        rows = rows.reshape(NE, MOST, f).astype(BF)
        packed[:, :, n * f:(n + 1) * f] = rows
        xg[0, 0:1, :, n * f:(n + 1) * f] = rows[0:1]

    pl.semaphore_wait(barrier, NE - 1 + NX * NC - 1)

    @pl.loop(1, NE)
    def _(j):
        copy(packed.at[j], xg.at[0, j], send_s.at[0], disp_r.at[j // PER], to_exp(j)).start()

    def rows_of(r):
        return pl.ds(r * PER, PER)

    def own_chunk(r):
        lo = 1 if r == 0 else r * PER
        part = xg.at[0, lo:(r + 1) * PER]
        got(part, disp_r.at[r])
        mine = xg.at[0, rows_of(r)]
        copy(mine, xg.at[2, rows_of(r)], send_s.at[1], ag_r.at[0, r], at_x(1)).start()
        copy(mine, xg.at[6, rows_of(r)], send_s.at[2], ag_r.at[1, r], at_x(3)).start()
        copy(mine, xg.at[1, rows_of(r)], send_s.at[3], core_r.at[0], at_x(0, 1)).start()

    hp = PER // 2

    def near_chunk(r):
        for n, (slot, step) in enumerate(((2, 1), (6, 3))):
            part = xg.at[slot, rows_of(r)]
            got(part, ag_r.at[n, r])
            lo = r * PER + n * hp
            copy(xg.at[slot, lo:lo + hp], xg.at[4, lo:lo + hp], send_s.at[4 + n], far_r.at[n, r], at_x(step)).start()
            copy(part, xg.at[slot + 1, rows_of(r)], send_s.at[6 + n], core_r.at[slot // 2], at_x(0, 1)).start()

    def far_chunk(r):
        for n in range(2):
            lo = r * PER + n * hp
            got(xg.at[4, lo:lo + hp], far_r.at[n, r])
        copy(xg.at[4, rows_of(r)], xg.at[5, rows_of(r)], send_s.at[8], core_r.at[2], at_x(0, 1)).start()

    h2 = wgu.shape[2]

    def front(k, first=False):
        for n in range(3):
            wcopies[3 * k + n].wait()
        xs = xg[k, :, :, 0:f].reshape(SLOTS, f)
        ds = xg[k, :, :, f:2 * f].reshape(SLOTS, f)
        gu = jnp.dot(xs, wgu[k], preferred_element_type=F32)
        bg = lax.dot_general(ds, wd[k], NT, preferred_element_type=F32)
        if first:
            acc[:, 0:h2] = gu
            acc[:, h2:] = bg
        else:
            acc[:, 0:h2] += gu
            acc[:, h2:] += bg

    own_chunk(0)
    own_chunk(1)
    near_chunk(0)
    own_chunk(2)
    near_chunk(1)
    own_chunk(3)
    near_chunk(2)
    front(0, True)
    far_chunk(0)
    near_chunk(3)
    got(xg.at[1], core_r.at[0])
    front(1)
    far_chunk(1)
    far_chunk(2)
    front(2)
    front(6)
    far_chunk(3)
    got(xg.at[3], core_r.at[1])
    front(3)
    got(xg.at[7], core_r.at[3])
    front(7)
    front(4)
    got(xg.at[5], core_r.at[2])
    front(5)

    h = h2 // 2
    pre_g = acc[:, 0:h]
    pre_u = acc[:, h:h2]
    back = acc[:, h2:]
    sig = 1.0 / (1.0 + jnp.exp(-pre_g))
    active = pre_g * sig
    gbuf[:, 0:h] = (back * pre_u * sig * (1.0 + pre_g * (1.0 - sig))).astype(BF)
    gbuf[:, h:h2] = (back * active).astype(BF)
    prod = active * pre_u * back
    part = lax.dot_general(jnp.ones((8, h), F32), prod, NT, preferred_element_type=F32,
                           precision=lax.Precision.HIGHEST)
    rpart[0] = part[0:1, :]
    for k in range(1, NX * NC):
        copy(rpart.at[0], rpart.at[k], send_s.at[9], rp_r, at_x(k // NC, k % NC)).start()

    def product(d, flip):
        k = ((NX - d) % NX) * NC + flip
        return lax.dot_general(gbuf[...], wgu[k], NT, preferred_element_type=F32)

    def share(d):
        ps[d] = product(d, 1).astype(BF)
        copy(ps.at[d], pb.at[d], send_s.at[10], pair_r.at[d], at_x(0, 1)).start()
        own[d] = product(d, 0)

    def paired(d):
        got(pb.at[d], pair_r.at[d])
        own[d] += pb[d].astype(F32)

    m = SLOTS // 2
    halves = (slice(0, m), slice(m, SLOTS))
    share(2)
    share(1)
    paired(2)
    snd[0] = own[2].astype(BF)
    for n, step in enumerate((1, 3)):
        copy(snd.at[0, halves[n]], relay.at[n], send_s.at[11 + n], rel_r.at[n], at_x(step)).start()
    share(3)
    paired(1)
    snd[1, halves[1]] = own[1, halves[1]].astype(BF)
    copy(snd.at[1, halves[1]], fin.at[0, halves[1]], send_s.at[13], fin_r.at[0, 1], at_x(1)).start()
    share(0)
    paired(3)
    snd[2, halves[0]] = own[3, halves[0]].astype(BF)
    copy(snd.at[2, halves[0]], fin.at[1, halves[0]], send_s.at[14], fin_r.at[1, 0], at_x(3)).start()
    for n, (slot, d) in enumerate(((1, 1), (2, 3))):
        got(relay.at[n], rel_r.at[n])
        snd[slot, halves[n]] = (own[d, halves[n]] + relay[n].astype(F32)).astype(BF)
        copy(snd.at[slot, halves[n]], fin.at[n, halves[n]], send_s.at[15 + n], fin_r.at[n, n], at_x(d)).start()
    paired(0)

    got(rpart.at[1:8], rp_r)
    total = rpart[0]
    for k in range(1, NX * NC):
        total = total + rpart[k]
    rtot[...] = total
    rret[0] = total

    @pl.loop(1, NE)
    def _(j):
        copy(rtot, rret.at[j], send_s.at[17], rr_r, from_exp(j)).start()

    for n in range(2):
        got(fin.at[0, halves[n]], fin_r.at[0, n])
        got(fin.at[1, halves[n]], fin_r.at[1, n])
        s = own[0, halves[n]] + fin[0, halves[n]].astype(F32) + fin[1, halves[n]].astype(F32)
        s = s.reshape(NE // 2, MOST, f).astype(BF)
        rets[n * (NE // 2):(n + 1) * (NE // 2)] = s
        if n == 0:
            ret[0:1] = s[0:1]

        @pl.loop(max(1, n * (NE // 2)), (n + 1) * (NE // 2))
        def _(j):
            copy(rets.at[j], ret.at[j], send_s.at[18], ret_r, from_exp(j)).start()

    got(rret.at[1:NE], rr_r)
    lane = lax.broadcasted_iota(jnp.int32, (NE, 1, SLOTS), 2) >> 3
    row = lax.broadcasted_iota(jnp.int32, (NE, 1, SLOTS), 0)
    by_slot = jnp.sum(jnp.where(lane == row, rret[...], 0.0), axis=0)
    by_token = jnp.dot(jnp.broadcast_to(by_slot, (8, SLOTS)), selbuf[...], preferred_element_type=F32,
                       precision=lax.Precision.HIGHEST)
    rg_out[...] = jnp.where(ids[pl.ds(seq, 1), :] < NE, by_token[0:1, :], 0.0)

    weight = jnp.sum(jnp.where(ids[...] < NE, rw[...], 0.0), axis=0, keepdims=True)
    scale = jnp.sum(selbuf[...] * weight, axis=1, keepdims=True)
    got(ret.at[1:NE], ret_r)
    rows = (ret[...].reshape(SLOTS, f).astype(F32) * scale).astype(BF)
    tg_out[...] = lax.dot_general(selbuf[...].astype(BF), rows, TN, preferred_element_type=F32).astype(BF)

    got(packed.at[1:NE], send_s.at[0])
    for n in range(1, 4):
        got(xg.at[0], send_s.at[n])
    for n in range(2):
        got(xg.at[0, 0:NE // 2], send_s.at[4 + n])
        got(xg.at[0], send_s.at[6 + n])
    got(xg.at[0], send_s.at[8])
    got(rpart.at[1:8], send_s.at[9])
    got(ps, send_s.at[10])
    for n in range(2):
        got(relay.at[n], send_s.at[11 + n])
        got(relay.at[n], send_s.at[13 + n])
        got(relay.at[n], send_s.at[15 + n])
    got(rret.at[1:NE], send_s.at[17])
    got(rets.at[1:NE], send_s.at[18])


def local(tokens, out_grad, expert_ids, route_weights, gate_proj, up_proj, down_proj):
    t, f = tokens.shape
    h = gate_proj.shape[2]
    vmem = pl.BlockSpec(memory_space=pltpu.VMEM)
    anym = pl.BlockSpec(memory_space=pl.ANY)
    dma = pltpu.SemaphoreType.DMA
    token_grad, route_grad = pl.pallas_call(
        kernel,
        out_shape=(jax.ShapeDtypeStruct((t, f), BF), jax.ShapeDtypeStruct((1, t), F32)),
        in_specs=[vmem] * 4 + [anym] * 3,
        out_specs=(vmem, vmem),
        scratch_shapes=[
            pltpu.VMEM((8, f, 2 * h), BF),
            pltpu.VMEM((8, h, f), BF),
            pltpu.VMEM((NE, MOST, 2 * f), BF),
            pltpu.VMEM((8, NE, MOST, 2 * f), BF),
            pltpu.VMEM((SLOTS, 3 * h), F32),
            pltpu.VMEM((SLOTS, 2 * h), BF),
            pltpu.VMEM((4, SLOTS, f), BF),
            pltpu.VMEM((4, SLOTS, f), BF),
            pltpu.VMEM((4, SLOTS, f), F32),
            pltpu.VMEM((2, SLOTS // 2, f), BF),
            pltpu.VMEM((3, SLOTS, f), BF),
            pltpu.VMEM((2, SLOTS, f), BF),
            pltpu.VMEM((NE, MOST, f), BF),
            pltpu.VMEM((NE, MOST, f), BF),
            pltpu.VMEM((SLOTS, t), F32),
            pltpu.VMEM((8, 1, SLOTS), F32),
            pltpu.VMEM((1, SLOTS), F32),
            pltpu.VMEM((NE, 1, SLOTS), F32),
            dma((8, 3)), dma((CHUNKS,)), dma((2, CHUNKS)), dma((2, CHUNKS)), dma((4,)),
            dma((4,)), dma((2,)), dma((2, 2)), dma(()), dma(()), dma(()), dma((19,)),
        ],
        compiler_params=pltpu.CompilerParams(
            collective_id=0, has_side_effects=True, vmem_limit_bytes=60 * 1024 * 1024),
        name="moe_back",
    )(tokens, out_grad, expert_ids.T, route_weights.T, gate_proj[0], up_proj[0], down_proj[0])
    return token_grad, route_grad.reshape(t, 1)


def solution(mesh):
    in_specs = (
        P("exp", "seq"),
        P("exp", "seq"),
        P("exp", None),
        P("exp", None),
        P("exp", None, "seq"),
        P("exp", None, "seq"),
        P("exp", "seq", None),
    )
    out_specs = (P("exp", "seq"), P("exp", "seq"))
    return jax.shard_map(local, mesh=mesh, in_specs=in_specs, out_specs=out_specs, check_vma=False)
```

```python
import jax
import jax.numpy as jnp
from jax import lax
from jax.experimental import pallas as pl
from jax.experimental.pallas import tpu as pltpu
from jax.sharding import PartitionSpec as P

MESH = pl.DeviceIdType.MESH
BF = jnp.bfloat16
F32 = jnp.float32
NX, NC, NY, NZ = 4, 2, 4, 8
NE = NY * NZ
MOST = 8
SLOTS = NE * MOST
DZ = (0, 1, 7, 4, 2, 6, 3, 5)
CHUNKS = len(DZ)
PER = NE // CHUNKS
GROUPS = 2
CPG = CHUNKS // GROUPS
ROWS = SLOTS // GROUPS
NT = (((1,), (1,)), ((), ()))
TN = (((0,), (0,)), ((), ()))


A, B = 0, 1
SCHEDULE = tuple(("send", n) for n in range(CHUNKS)) + (
    ("own", 0), ("own", 1), ("own", 2), ("near", 0), ("near", 1), ("near", 2), ("own", 3), ("far", 0), ("near", 3),
    ("far", 1), ("far", 2), ("own", 4), ("own", 5), ("front", A, 0), ("far", 3),
    ("front", A, 1), ("front", A, 2), ("front", A, 6), ("near", 4), ("near", 5), ("own", 6), ("own", 7),
    ("front", A, 3), ("front", A, 7), ("front", A, 4), ("front", A, 5), ("middle", A),
    ("out", A, 2), ("mine", A, 2), ("out", A, 1), ("near", 6), ("paired", A, 2), ("mine", A, 1), ("far", 4),
    ("out", A, 3), ("paired", A, 1), ("near", 7), ("mine", A, 3), ("far", 5), ("out", A, 0), ("paired", A, 3),
    ("mine", A, 0), ("far", 6), ("front", B, 0), ("front", B, 1), ("front", B, 2), ("front", B, 6),
    ("front", B, 3), ("front", B, 7), ("far", 7), ("front", B, 4), ("relayed", A), ("front", B, 5), ("middle", B),
    ("route_parts",),
    ("out", B, 2), ("mine", B, 2), ("out", B, 1), ("paired", B, 2), ("mine", B, 1), ("out", B, 3), ("paired", B, 1),
    ("mine", B, 3), ("out", B, 0), ("paired", B, 3), ("mine", B, 0), ("paired", A, 0), ("finished", A),
    ("paired", B, 0), ("route_back",), ("relayed", B), ("finished", B),
)


def kernel(tok, og, ids, rw, wg_h, wu_h, wd_h, tg_out, rg_out,
           wgu, wd, packed, xg, acc, gbuf, ps, pb, own, relay, snd, fin, rets, ret,
           selbuf, rpart, rtot, rret,
           wsem, disp_r, ag_r, far_r, core_r, pair_r, rel_r, fin_r, ret_r, rp_r, rr_r, send_s):
    seq, exp = lax.axis_index("seq"), lax.axis_index("exp")
    x, c = seq // NC, seq % NC
    y, z = exp // NZ, exp % NZ
    f = tok.shape[1]

    def at_x(step, flip=0):
        return {"seq": NC * ((x + step) % NX) + (c + flip) % NC}

    def to_exp(i, dy):
        return {"exp": ((y + dy) % NY) * NZ + (z + DZ[i]) % NZ}

    def from_exp(i, dy):
        return {"exp": ((y + NY - dy) % NY) * NZ + (z + NZ - DZ[i]) % NZ}

    def copy(src, dst, ssem, rsem, dev):
        return pltpu.make_async_remote_copy(
            src_ref=src, dst_ref=dst, send_sem=ssem, recv_sem=rsem,
            device_id=dev, device_id_type=MESH)

    def got(ref, sem):
        pltpu.make_async_copy(ref, ref, sem).wait()

    wcopies = []
    for k in range(NX * NC):
        dx, flip = k // NC, k % NC
        first = pl.multiple_of((NC * ((x + NX - dx) % NX) + (c + flip) % NC) * f, 128)
        h = wg_h.shape[1]
        for n, (src, dst) in enumerate((
                (wg_h.at[pl.ds(first, f), :], wgu.at[k, :, 0:h]),
                (wu_h.at[pl.ds(first, f), :], wgu.at[k, :, h:2 * h]),
                (wd_h.at[:, pl.ds(first, f)], wd.at[k]))):
            one = pltpu.make_async_copy(src, dst, wsem.at[k, n])
            one.start()
            wcopies.append(one)

    barrier = pltpu.get_barrier_semaphore()

    for n in range(CHUNKS):
        @pl.loop(1 if n == 0 else 0, NY)
        def _(dy):
            pl.semaphore_signal(barrier, inc=1, device_id=to_exp(n, dy), device_id_type=MESH)

    for k in range(1, NX * NC):
        pl.semaphore_signal(barrier, inc=1, device_id=at_x(k // NC, k % NC), device_id_type=MESH)

    q = lax.broadcasted_iota(jnp.int32, (SLOTS, tok.shape[0]), 0)
    j = q >> 3
    i = j >> 2
    dz = jnp.zeros_like(i)
    for n in range(1, CHUNKS):
        dz = jnp.where(i == n, DZ[n], dz)
    wanted = ((y + (j & 3)) & 3) * NZ + ((z + dz) & 7)
    hot = ids[0:1, :] == wanted
    for k in range(1, ids.shape[0]):
        hot = hot | (ids[k:k + 1, :] == wanted)
    hot = jnp.where(hot, 1.0, 0.0)
    t0 = lax.broadcasted_iota(jnp.int32, (tok.shape[0], tok.shape[0]), 0)
    t1 = lax.broadcasted_iota(jnp.int32, (tok.shape[0], tok.shape[0]), 1)
    before = jnp.where(t0 < t1, 1.0, 0.0).astype(BF)
    rank = jnp.dot(hot.astype(BF), before, preferred_element_type=F32)
    sel = jnp.where(rank == (q & 7).astype(F32), hot, 0.0)
    selbuf[...] = sel
    selb = sel.astype(BF)
    for n, src in enumerate((tok, og)):
        rows = jnp.dot(selb, src[...], preferred_element_type=F32)
        rows = rows.reshape(NE, MOST, f).astype(BF)
        packed[:, :, n * f:(n + 1) * f] = rows
        xg[0, 0:1, :, n * f:(n + 1) * f] = rows[0:1]

    pl.semaphore_wait(barrier, NE - 1 + NX * NC - 1)

    def send(n):
        @pl.loop(1 if n == 0 else 0, NY)
        def _(dy):
            j = n * PER + dy
            copy(packed.at[j], xg.at[0, j], send_s.at[0], disp_r.at[n], to_exp(n, dy)).start()

    def rows_of(r):
        return pl.ds(r * PER, PER)

    def own_chunk(r):
        lo = 1 if r == 0 else r * PER
        got(xg.at[0, lo:(r + 1) * PER], disp_r.at[r])
        mine = xg.at[0, rows_of(r)]
        copy(mine, xg.at[2, rows_of(r)], send_s.at[1], ag_r.at[0, r], at_x(1)).start()
        copy(mine, xg.at[6, rows_of(r)], send_s.at[2], ag_r.at[1, r], at_x(3)).start()
        copy(mine, xg.at[1, rows_of(r)], send_s.at[3], core_r.at[0, r // CPG], at_x(0, 1)).start()

    hp = PER // 2

    def near_chunk(r):
        for n, (slot, step) in enumerate(((2, 1), (6, 3))):
            part = xg.at[slot, rows_of(r)]
            got(part, ag_r.at[n, r])
            lo = r * PER + n * hp
            copy(xg.at[slot, lo:lo + hp], xg.at[4, lo:lo + hp], send_s.at[4 + n], far_r.at[n, r], at_x(step)).start()
            copy(part, xg.at[slot + 1, rows_of(r)], send_s.at[6 + n], core_r.at[slot // 2, r // CPG], at_x(0, 1)).start()

    def far_chunk(r):
        for n in range(2):
            lo = r * PER + n * hp
            got(xg.at[4, lo:lo + hp], far_r.at[n, r])
        copy(xg.at[4, rows_of(r)], xg.at[5, rows_of(r)], send_s.at[8], core_r.at[2, r // CPG], at_x(0, 1)).start()

    h2 = wgu.shape[2]

    def front(g, k):
        if g == 0:
            for n in range(3):
                wcopies[3 * k + n].wait()
        blocks = slice(g * CPG * PER, (g + 1) * CPG * PER)
        rows = slice(g * ROWS, (g + 1) * ROWS)
        if k % 2:
            got(xg.at[k, blocks], core_r.at[k // 2, g])
        xs = xg[k, blocks, :, 0:f].reshape(ROWS, f)
        ds = xg[k, blocks, :, f:2 * f].reshape(ROWS, f)
        gu = jnp.dot(xs, wgu[k], preferred_element_type=F32)
        bg = lax.dot_general(ds, wd[k], NT, preferred_element_type=F32)
        if k == 0:
            acc[rows, 0:h2] = gu
            acc[rows, h2:] = bg
        else:
            acc[rows, 0:h2] += gu
            acc[rows, h2:] += bg

    h = h2 // 2

    def middle(g):
        rows = slice(g * ROWS, (g + 1) * ROWS)
        pre_g = acc[rows, 0:h]
        pre_u = acc[rows, h:h2]
        back = acc[rows, h2:]
        sig = 1.0 / (1.0 + jnp.exp(-pre_g))
        active = pre_g * sig
        gbuf[rows, 0:h] = (back * pre_u * sig * (1.0 + pre_g * (1.0 - sig))).astype(BF)
        gbuf[rows, h:h2] = (back * active).astype(BF)
        part = lax.dot_general(jnp.ones((8, h), F32), active * pre_u * back, NT, preferred_element_type=F32,
                               precision=lax.Precision.HIGHEST)
        rpart[0, :, rows] = part[0:1, :]

    def product(g, d, flip):
        k = ((NX - d) % NX) * NC + flip
        return lax.dot_general(gbuf[g * ROWS:(g + 1) * ROWS], wgu[k], NT, preferred_element_type=F32)

    m = ROWS // 2

    def half(g, n):
        return slice(g * ROWS + n * m, g * ROWS + (n + 1) * m)

    def out(g, d):
        rows = slice(g * ROWS, (g + 1) * ROWS)
        ps[d, rows] = product(g, d, 1).astype(BF)
        copy(ps.at[d, rows], pb.at[d, rows], send_s.at[10], pair_r.at[d, g], at_x(0, 1)).start()

    def mine(g, d):
        own[d, g * ROWS:(g + 1) * ROWS] = product(g, d, 0)

    def paired(g, d):
        rows = slice(g * ROWS, (g + 1) * ROWS)
        got(pb.at[d, rows], pair_r.at[d, g])
        if d == 0:
            own[0, rows] += pb[0, rows].astype(F32)
        elif d == 2:
            snd[0, rows] = (own[2, rows] + pb[2, rows].astype(F32)).astype(BF)
            for n, step in enumerate((1, 3)):
                copy(snd.at[0, half(g, n)], relay.at[n, g], send_s.at[11 + n], rel_r.at[n, g], at_x(step)).start()
        else:
            n = 0 if d == 1 else 1
            own[d, rows] += pb[d, rows].astype(F32)
            other = half(g, 1 - n)
            snd[1 + n, other] = own[d, other].astype(BF)
            copy(snd.at[1 + n, other], fin.at[n, other], send_s.at[13 + n], fin_r.at[n, 1 - n, g], at_x(d)).start()

    def relayed(g):
        for n, d in enumerate((1, 3)):
            got(relay.at[n, g], rel_r.at[n, g])
            this = half(g, n)
            snd[1 + n, this] = (own[d, this] + relay[n, g].astype(F32)).astype(BF)
            copy(snd.at[1 + n, this], fin.at[n, this], send_s.at[15 + n], fin_r.at[n, n, g], at_x(d)).start()

    def finished(g):
        for n in (1, 0):
            this = half(g, n)
            got(fin.at[0, this], fin_r.at[0, n, g])
            got(fin.at[1, this], fin_r.at[1, n, g])
            s = own[0, this] + fin[0, this].astype(F32) + fin[1, this].astype(F32)
            s = s.reshape(m // MOST, MOST, f).astype(BF)
            lo = (g * ROWS + n * m) // MOST
            rets[lo:lo + m // MOST] = s
            if lo == 0:
                ret[0:1] = s[0:1]
            for r in reversed(range(lo // PER, (lo + m // MOST) // PER)):
                @pl.loop(1 if r == 0 else 0, NY)
                def _(dy):
                    j = r * PER + dy
                    copy(rets.at[j], ret.at[j], send_s.at[18], ret_r, from_exp(r, dy)).start()

    def route_parts():
        for k in range(1, NX * NC):
            copy(rpart.at[0], rpart.at[k], send_s.at[9], rp_r, at_x(k // NC, k % NC)).start()

    def route_back():
        got(rpart.at[1:8], rp_r)
        total = rpart[0]
        for k in range(1, NX * NC):
            total = total + rpart[k]
        rtot[...] = total
        rret[0] = total
        for r in range(CHUNKS):
            @pl.loop(1 if r == 0 else 0, NY)
            def _(dy):
                copy(rtot, rret.at[r * PER + dy], send_s.at[17], rr_r, from_exp(r, dy)).start()

    step_of = {"own": own_chunk, "near": near_chunk, "far": far_chunk, "front": front, "middle": middle,
               "out": out, "mine": mine, "send": send, "paired": paired, "relayed": relayed, "finished": finished,
               "route_parts": route_parts, "route_back": route_back}
    for step in SCHEDULE:
        step_of[step[0]](*step[1:])

    got(rret.at[1:NE], rr_r)
    lane = lax.broadcasted_iota(jnp.int32, (NE, 1, SLOTS), 2) >> 3
    row = lax.broadcasted_iota(jnp.int32, (NE, 1, SLOTS), 0)
    by_slot = jnp.sum(jnp.where(lane == row, rret[...], 0.0), axis=0)
    by_token = jnp.dot(jnp.broadcast_to(by_slot, (8, SLOTS)), selbuf[...], preferred_element_type=F32,
                       precision=lax.Precision.HIGHEST)
    rg_out[...] = jnp.where(ids[pl.ds(seq, 1), :] < NE, by_token[0:1, :], 0.0)

    weight = jnp.sum(jnp.where(ids[...] < NE, rw[...], 0.0), axis=0, keepdims=True)
    scale = jnp.sum(selbuf[...] * weight, axis=1, keepdims=True)
    got(ret.at[1:NE], ret_r)
    rows = (ret[...].reshape(SLOTS, f).astype(F32) * scale).astype(BF)
    tg_out[...] = lax.dot_general(selbuf[...].astype(BF), rows, TN, preferred_element_type=F32).astype(BF)

    got(packed.at[1:NE], send_s.at[0])
    for n in range(1, 4):
        got(xg.at[0], send_s.at[n])
    for n in range(2):
        got(xg.at[0, 0:NE // 2], send_s.at[4 + n])
        got(xg.at[0], send_s.at[6 + n])
    got(xg.at[0], send_s.at[8])
    got(rpart.at[1:8], send_s.at[9])
    got(ps, send_s.at[10])
    for n in range(11, 17):
        got(relay.at[0], send_s.at[n])
    got(rret.at[1:NE], send_s.at[17])
    got(rets.at[1:NE], send_s.at[18])


def local(tokens, out_grad, expert_ids, route_weights, gate_proj, up_proj, down_proj):
    t, f = tokens.shape
    h = gate_proj.shape[2]
    vmem = pl.BlockSpec(memory_space=pltpu.VMEM)
    anym = pl.BlockSpec(memory_space=pl.ANY)
    dma = pltpu.SemaphoreType.DMA
    token_grad, route_grad = pl.pallas_call(
        kernel,
        out_shape=(jax.ShapeDtypeStruct((t, f), BF), jax.ShapeDtypeStruct((1, t), F32)),
        in_specs=[vmem] * 4 + [anym] * 3,
        out_specs=(vmem, vmem),
        scratch_shapes=[
            pltpu.VMEM((8, f, 2 * h), BF),
            pltpu.VMEM((8, h, f), BF),
            pltpu.VMEM((NE, MOST, 2 * f), BF),
            pltpu.VMEM((8, NE, MOST, 2 * f), BF),
            pltpu.VMEM((SLOTS, 3 * h), F32),
            pltpu.VMEM((SLOTS, 2 * h), BF),
            pltpu.VMEM((4, SLOTS, f), BF),
            pltpu.VMEM((4, SLOTS, f), BF),
            pltpu.VMEM((4, SLOTS, f), F32),
            pltpu.VMEM((2, GROUPS, ROWS // 2, f), BF),
            pltpu.VMEM((3, SLOTS, f), BF),
            pltpu.VMEM((2, SLOTS, f), BF),
            pltpu.VMEM((NE, MOST, f), BF),
            pltpu.VMEM((NE, MOST, f), BF),
            pltpu.VMEM((SLOTS, t), F32),
            pltpu.VMEM((8, 1, SLOTS), F32),
            pltpu.VMEM((1, SLOTS), F32),
            pltpu.VMEM((NE, 1, SLOTS), F32),
            dma((8, 3)), dma((CHUNKS,)), dma((2, CHUNKS)), dma((2, CHUNKS)), dma((4, GROUPS)),
            dma((4, GROUPS)), dma((2, GROUPS)), dma((2, 2, GROUPS)), dma(()), dma(()), dma(()), dma((19,)),
        ],
        compiler_params=pltpu.CompilerParams(
            collective_id=0, has_side_effects=True, vmem_limit_bytes=60 * 1024 * 1024),
        name="moe_back",
    )(tokens, out_grad, expert_ids.T, route_weights.T, gate_proj[0], up_proj[0], down_proj[0])
    return token_grad, route_grad.reshape(t, 1)


def solution(mesh):
    in_specs = (
        P("exp", "seq"),
        P("exp", "seq"),
        P("exp", None),
        P("exp", None),
        P("exp", None, "seq"),
        P("exp", None, "seq"),
        P("exp", "seq", None),
    )
    out_specs = (P("exp", "seq"), P("exp", "seq"))
    return jax.shard_map(local, mesh=mesh, in_specs=in_specs, out_specs=out_specs, check_vma=False)
```

```python
import jax
import jax.numpy as jnp
from jax import lax
from jax.experimental import pallas as pl
from jax.experimental.pallas import tpu as pltpu
from jax.sharding import PartitionSpec as P

MESH = pl.DeviceIdType.MESH
BF = jnp.bfloat16
F32 = jnp.float32
NX, NC, NY, NZ = 4, 2, 4, 8
NE = NY * NZ
MOST = 8
SLOTS = NE * MOST
DZ = (0, 1, 7, 2, 6, 3, 5, 4)
BOUND = (0, 5, 8)
CHUNKS = len(DZ)
PER = NE // CHUNKS
GROUPS = len(BOUND) - 1
STEP = PER * MOST
NT = (((1,), (1,)), ((), ()))
TN = (((0,), (0,)), ((), ()))


A, B = 0, 1
SCHEDULE = (
    ("send", 0), ("signal", 0), ("known", 0), ("signal", 1), ("send", 1), ("send", 2), ("own", 0), ("known", 1),
    ("signal", 2), ("send", 3), ("send", 4), ("known", 2), ("signal", 3), ("own", 1), ("own", 2), ("known", 3),
    ("send", 5), ("send", 6), ("send", 7),
    ("near", 0), ("near", 1), ("near", 2), ("own", 3), ("own", 4), ("far", 0), ("far", 1), ("far", 2),
    ("front", A, 0), ("near", 3), ("near", 4), ("front", A, 1), ("own", 5), ("own", 6), ("far", 3), ("far", 4),
    ("front", A, 2), ("front", A, 6), ("own", 7), ("front", A, 3), ("front", A, 7), ("front", A, 4),
    ("front", A, 5), ("middle", A),
    ("out", A, 2), ("mine", A, 2), ("near", 5), ("out", A, 1), ("paired", A, 2), ("near", 6), ("mine", A, 1),
    ("out", A, 3), ("paired", A, 1), ("near", 7), ("mine", A, 3), ("far", 5), ("out", A, 0), ("paired", A, 3),
    ("mine", A, 0), ("far", 6), ("front", B, 0), ("front", B, 1), ("front", B, 2), ("front", B, 6), ("relayed", A),
    ("front", B, 3), ("front", B, 7), ("far", 7), ("front", B, 4), ("front", B, 5), ("middle", B), ("route_parts",),
    ("out", B, 2), ("mine", B, 2), ("out", B, 1), ("paired", B, 2), ("mine", B, 1), ("out", B, 3), ("paired", B, 1),
    ("mine", B, 3), ("out", B, 0), ("paired", B, 3), ("mine", B, 0), ("paired", A, 0), ("finished", A),
    ("paired", B, 0), ("route_back",), ("relayed", B), ("finished", B),
)


def kernel(tok, og, ids, rw, wg_h, wu_h, wd_h, tg_out, rg_out,
           wgu, wd, packed, xg, acc, gbuf, ps, pb, own, relay, snd, fin, rets, ret,
           selbuf, rpart, rtot, rret,
           wsem, disp_r, ag_r, far_r, core_r, pair_r, rel_r, fin_r, ret_r, rp_r, rr_r, send_s, level_s):
    seq, exp = lax.axis_index("seq"), lax.axis_index("exp")
    x, c = seq // NC, seq % NC
    y, z = exp // NZ, exp % NZ
    f = tok.shape[1]

    def at_x(step, flip=0):
        return {"seq": NC * ((x + step) % NX) + (c + flip) % NC}

    def to_exp(i, dy):
        return {"exp": ((y + dy) % NY) * NZ + (z + DZ[i]) % NZ}

    def from_exp(i, dy):
        return {"exp": ((y + NY - dy) % NY) * NZ + (z + NZ - DZ[i]) % NZ}

    def copy(src, dst, ssem, rsem, dev):
        return pltpu.make_async_remote_copy(
            src_ref=src, dst_ref=dst, send_sem=ssem, recv_sem=rsem,
            device_id=dev, device_id_type=MESH)

    def got(ref, sem):
        pltpu.make_async_copy(ref, ref, sem).wait()

    wcopies = []
    for k in range(NX * NC):
        dx, flip = k // NC, k % NC
        first = pl.multiple_of((NC * ((x + NX - dx) % NX) + (c + flip) % NC) * f, 128)
        h = wg_h.shape[1]
        for n, (src, dst) in enumerate((
                (wg_h.at[pl.ds(first, f), :], wgu.at[k, :, 0:h]),
                (wu_h.at[pl.ds(first, f), :], wgu.at[k, :, h:2 * h]),
                (wd_h.at[:, pl.ds(first, f)], wd.at[k]))):
            one = pltpu.make_async_copy(src, dst, wsem.at[k, n])
            one.start()
            wcopies.append(one)

    barrier = pltpu.get_barrier_semaphore()

    def at_z(step):
        return {"exp": y * NZ + (z + step) % NZ}

    for dy in range(1, NY):
        pl.semaphore_signal(barrier, inc=1, device_id=to_exp(0, dy), device_id_type=MESH)
    for step in (1, NZ - 1):
        pl.semaphore_signal(barrier, inc=1, device_id=at_z(step), device_id_type=MESH)
    for k in range(1, NX * NC):
        pl.semaphore_signal(barrier, inc=1, device_id=at_x(k // NC, k % NC), device_id_type=MESH)

    q = lax.broadcasted_iota(jnp.int32, (SLOTS, tok.shape[0]), 0)
    j = q >> 3
    i = j >> 2
    dz = jnp.zeros_like(i)
    for n in range(1, CHUNKS):
        dz = jnp.where(i == n, DZ[n], dz)
    wanted = ((y + (j & 3)) & 3) * NZ + ((z + dz) & 7)
    hot = ids[0:1, :] == wanted
    for k in range(1, ids.shape[0]):
        hot = hot | (ids[k:k + 1, :] == wanted)
    hot = jnp.where(hot, 1.0, 0.0)
    t0 = lax.broadcasted_iota(jnp.int32, (tok.shape[0], tok.shape[0]), 0)
    t1 = lax.broadcasted_iota(jnp.int32, (tok.shape[0], tok.shape[0]), 1)
    before = jnp.where(t0 < t1, 1.0, 0.0).astype(BF)
    rank = jnp.dot(hot.astype(BF), before, preferred_element_type=F32)
    sel = jnp.where(rank == (q & 7).astype(F32), hot, 0.0)
    selbuf[...] = sel
    selb = sel.astype(BF)
    for n, src in enumerate((tok, og)):
        rows = jnp.dot(selb, src[...], preferred_element_type=F32)
        rows = rows.reshape(NE, MOST, f).astype(BF)
        packed[:, :, n * f:(n + 1) * f] = rows
        xg[0, 0:1, :, n * f:(n + 1) * f] = rows[0:1]

    pl.semaphore_wait(barrier, NY - 1 + 2 + NX * NC - 1)

    def send(n):
        @pl.loop(1 if n == 0 else 0, NY)
        def _(dy):
            j = n * PER + dy
            copy(packed.at[j], xg.at[0, j], send_s.at[0], disp_r.at[n], to_exp(n, dy)).start()

    def signal(n):
        for step in (1, NZ - 1):
            pl.semaphore_signal(level_s.at[n], inc=1, device_id=at_z(step), device_id_type=MESH)

    def known(n):
        pl.semaphore_wait(level_s.at[n], 2)

    def group_of(r):
        return sum(r >= b for b in BOUND[1:-1])

    def group(g):
        return slice(BOUND[g] * STEP, BOUND[g + 1] * STEP)

    def size(g):
        return (BOUND[g + 1] - BOUND[g]) * STEP

    def rows_of(r):
        return pl.ds(r * PER, PER)

    def own_chunk(r):
        lo = 1 if r == 0 else r * PER
        got(xg.at[0, lo:(r + 1) * PER], disp_r.at[r])
        mine = xg.at[0, rows_of(r)]
        copy(mine, xg.at[2, rows_of(r)], send_s.at[1], ag_r.at[0, r], at_x(1)).start()
        copy(mine, xg.at[6, rows_of(r)], send_s.at[2], ag_r.at[1, r], at_x(3)).start()
        copy(mine, xg.at[1, rows_of(r)], send_s.at[3], core_r.at[0, group_of(r)], at_x(0, 1)).start()

    hp = PER // 2

    def near_chunk(r):
        for n, (slot, step) in enumerate(((2, 1), (6, 3))):
            part = xg.at[slot, rows_of(r)]
            got(part, ag_r.at[n, r])
            lo = r * PER + n * hp
            copy(xg.at[slot, lo:lo + hp], xg.at[4, lo:lo + hp], send_s.at[4 + n], far_r.at[n, r], at_x(step)).start()
            copy(part, xg.at[slot + 1, rows_of(r)], send_s.at[6 + n], core_r.at[slot // 2, group_of(r)], at_x(0, 1)).start()

    def far_chunk(r):
        for n in range(2):
            lo = r * PER + n * hp
            got(xg.at[4, lo:lo + hp], far_r.at[n, r])
        copy(xg.at[4, rows_of(r)], xg.at[5, rows_of(r)], send_s.at[8], core_r.at[2, group_of(r)], at_x(0, 1)).start()

    h2 = wgu.shape[2]

    def front(g, k):
        for n in range(3):
            if wcopies[3 * k + n] is not None:
                wcopies[3 * k + n].wait()
                wcopies[3 * k + n] = None
        blocks = slice(BOUND[g] * PER, BOUND[g + 1] * PER)
        rows = group(g)
        if k % 2:
            got(xg.at[k, blocks], core_r.at[k // 2, g])
        xs = xg[k, blocks, :, 0:f].reshape(size(g), f)
        ds = xg[k, blocks, :, f:2 * f].reshape(size(g), f)
        gu = jnp.dot(xs, wgu[k], preferred_element_type=F32)
        bg = lax.dot_general(ds, wd[k], NT, preferred_element_type=F32)
        if k == 0:
            acc[rows, 0:h2] = gu
            acc[rows, h2:] = bg
        else:
            acc[rows, 0:h2] += gu
            acc[rows, h2:] += bg

    h = h2 // 2

    def middle(g):
        rows = group(g)
        pre_g = acc[rows, 0:h]
        pre_u = acc[rows, h:h2]
        back = acc[rows, h2:]
        sig = 1.0 / (1.0 + jnp.exp(-pre_g))
        active = pre_g * sig
        gbuf[rows, 0:h] = (back * pre_u * sig * (1.0 + pre_g * (1.0 - sig))).astype(BF)
        gbuf[rows, h:h2] = (back * active).astype(BF)
        part = lax.dot_general(jnp.ones((8, h), F32), active * pre_u * back, NT, preferred_element_type=F32,
                               precision=lax.Precision.HIGHEST)
        rpart[0, :, rows] = part[0:1, :]

    def product(g, d, flip):
        k = ((NX - d) % NX) * NC + flip
        return lax.dot_general(gbuf[group(g)], wgu[k], NT, preferred_element_type=F32)

    def half(g, n):
        first, m = BOUND[g] * STEP, size(g) // 2
        return slice(first + n * m, first + (n + 1) * m)

    def passing(g):
        return slice(BOUND[g] * STEP // 2, BOUND[g + 1] * STEP // 2)

    def out(g, d):
        rows = group(g)
        ps[d, rows] = product(g, d, 1).astype(BF)
        copy(ps.at[d, rows], pb.at[d, rows], send_s.at[10], pair_r.at[d, g], at_x(0, 1)).start()

    def mine(g, d):
        own[d, group(g)] = product(g, d, 0)

    def paired(g, d):
        rows = group(g)
        got(pb.at[d, rows], pair_r.at[d, g])
        if d == 0:
            own[0, rows] += pb[0, rows].astype(F32)
        elif d == 2:
            snd[0, rows] = (own[2, rows] + pb[2, rows].astype(F32)).astype(BF)
            for n, step in enumerate((1, 3)):
                copy(snd.at[0, half(g, n)], relay.at[n, passing(g)], send_s.at[11 + n], rel_r.at[n, g], at_x(step)).start()
        else:
            n = 0 if d == 1 else 1
            own[d, rows] += pb[d, rows].astype(F32)
            other = half(g, 1 - n)
            snd[1 + n, other] = own[d, other].astype(BF)
            copy(snd.at[1 + n, other], fin.at[n, other], send_s.at[13 + n], fin_r.at[n, 1 - n, g], at_x(d)).start()

    def relayed(g):
        for n, d in enumerate((1, 3)):
            got(relay.at[n, passing(g)], rel_r.at[n, g])
            this = half(g, n)
            snd[1 + n, this] = (own[d, this] + relay[n, passing(g)].astype(F32)).astype(BF)
            copy(snd.at[1 + n, this], fin.at[n, this], send_s.at[15 + n], fin_r.at[n, n, g], at_x(d)).start()

    def finished(g):
        for n in (1, 0):
            this = half(g, n)
            got(fin.at[0, this], fin_r.at[0, n, g])
            got(fin.at[1, this], fin_r.at[1, n, g])
            s = own[0, this] + fin[0, this].astype(F32) + fin[1, this].astype(F32)
            lo, hi = this.start // MOST, this.stop // MOST
            s = s.reshape(hi - lo, MOST, f).astype(BF)
            rets[lo:hi] = s
            if lo == 0:
                ret[0:1] = s[0:1]
            for r in range(CHUNKS):
                first, last = max(lo, r * PER, 1) - r * PER, min(hi, (r + 1) * PER) - r * PER
                if first >= last:
                    continue

                @pl.loop(first, last)
                def _(dy):
                    j = r * PER + dy
                    copy(rets.at[j], ret.at[j], send_s.at[18], ret_r, from_exp(r, dy)).start()

    def route_parts():
        for k in range(1, NX * NC):
            copy(rpart.at[0], rpart.at[k], send_s.at[9], rp_r, at_x(k // NC, k % NC)).start()

    def route_back():
        got(rpart.at[1:8], rp_r)
        total = rpart[0]
        for k in range(1, NX * NC):
            total = total + rpart[k]
        rtot[...] = total
        rret[0] = total
        for r in range(CHUNKS):
            @pl.loop(1 if r == 0 else 0, NY)
            def _(dy):
                copy(rtot, rret.at[r * PER + dy], send_s.at[17], rr_r, from_exp(r, dy)).start()

    step_of = {"own": own_chunk, "near": near_chunk, "far": far_chunk, "front": front, "middle": middle,
               "out": out, "mine": mine, "send": send, "signal": signal, "known": known, "paired": paired, "relayed": relayed, "finished": finished,
               "route_parts": route_parts, "route_back": route_back}
    for step in SCHEDULE:
        step_of[step[0]](*step[1:])

    got(rret.at[1:NE], rr_r)
    lane = lax.broadcasted_iota(jnp.int32, (NE, 1, SLOTS), 2) >> 3
    row = lax.broadcasted_iota(jnp.int32, (NE, 1, SLOTS), 0)
    by_slot = jnp.sum(jnp.where(lane == row, rret[...], 0.0), axis=0)
    by_token = jnp.dot(jnp.broadcast_to(by_slot, (8, SLOTS)), selbuf[...], preferred_element_type=F32,
                       precision=lax.Precision.HIGHEST)
    rg_out[...] = jnp.where(ids[pl.ds(seq, 1), :] < NE, by_token[0:1, :], 0.0)

    weight = jnp.sum(jnp.where(ids[...] < NE, rw[...], 0.0), axis=0, keepdims=True)
    scale = jnp.sum(selbuf[...] * weight, axis=1, keepdims=True)
    got(ret.at[1:NE], ret_r)
    rows = (ret[...].reshape(SLOTS, f).astype(F32) * scale).astype(BF)
    tg_out[...] = lax.dot_general(selbuf[...].astype(BF), rows, TN, preferred_element_type=F32).astype(BF)

    got(packed.at[1:NE], send_s.at[0])
    for n in range(1, 4):
        got(xg.at[0], send_s.at[n])
    for n in range(2):
        got(xg.at[0, 0:NE // 2], send_s.at[4 + n])
        got(xg.at[0], send_s.at[6 + n])
    got(xg.at[0], send_s.at[8])
    got(rpart.at[1:8], send_s.at[9])
    got(ps, send_s.at[10])
    for n in range(11, 17):
        got(relay.at[0], send_s.at[n])
    got(rret.at[1:NE], send_s.at[17])
    got(rets.at[1:NE], send_s.at[18])


def local(tokens, out_grad, expert_ids, route_weights, gate_proj, up_proj, down_proj):
    t, f = tokens.shape
    h = gate_proj.shape[2]
    vmem = pl.BlockSpec(memory_space=pltpu.VMEM)
    anym = pl.BlockSpec(memory_space=pl.ANY)
    dma = pltpu.SemaphoreType.DMA
    token_grad, route_grad = pl.pallas_call(
        kernel,
        out_shape=(jax.ShapeDtypeStruct((t, f), BF), jax.ShapeDtypeStruct((1, t), F32)),
        in_specs=[vmem] * 4 + [anym] * 3,
        out_specs=(vmem, vmem),
        scratch_shapes=[
            pltpu.VMEM((8, f, 2 * h), BF),
            pltpu.VMEM((8, h, f), BF),
            pltpu.VMEM((NE, MOST, 2 * f), BF),
            pltpu.VMEM((8, NE, MOST, 2 * f), BF),
            pltpu.VMEM((SLOTS, 3 * h), F32),
            pltpu.VMEM((SLOTS, 2 * h), BF),
            pltpu.VMEM((4, SLOTS, f), BF),
            pltpu.VMEM((4, SLOTS, f), BF),
            pltpu.VMEM((4, SLOTS, f), F32),
            pltpu.VMEM((2, SLOTS // 2, f), BF),
            pltpu.VMEM((3, SLOTS, f), BF),
            pltpu.VMEM((2, SLOTS, f), BF),
            pltpu.VMEM((NE, MOST, f), BF),
            pltpu.VMEM((NE, MOST, f), BF),
            pltpu.VMEM((SLOTS, t), F32),
            pltpu.VMEM((8, 1, SLOTS), F32),
            pltpu.VMEM((1, SLOTS), F32),
            pltpu.VMEM((NE, 1, SLOTS), F32),
            dma((8, 3)), dma((CHUNKS,)), dma((2, CHUNKS)), dma((2, CHUNKS)), dma((4, GROUPS)),
            dma((4, GROUPS)), dma((2, GROUPS)), dma((2, 2, GROUPS)), dma(()), dma(()), dma(()), dma((19,)),
            pltpu.SemaphoreType.REGULAR((4,)),
        ],
        compiler_params=pltpu.CompilerParams(
            collective_id=0, has_side_effects=True, vmem_limit_bytes=60 * 1024 * 1024),
        name="moe_back",
    )(tokens, out_grad, expert_ids.T, route_weights.T, gate_proj[0], up_proj[0], down_proj[0])
    return token_grad, route_grad.reshape(t, 1)


def solution(mesh):
    in_specs = (
        P("exp", "seq"),
        P("exp", "seq"),
        P("exp", None),
        P("exp", None),
        P("exp", None, "seq"),
        P("exp", None, "seq"),
        P("exp", "seq", None),
    )
    out_specs = (P("exp", "seq"), P("exp", "seq"))
    return jax.shard_map(local, mesh=mesh, in_specs=in_specs, out_specs=out_specs, check_vma=False)
```

```python
import jax
import jax.numpy as jnp
from jax import lax
from jax.experimental import pallas as pl
from jax.experimental.pallas import tpu as pltpu
from jax.sharding import PartitionSpec as P

MESH = pl.DeviceIdType.MESH
BF = jnp.bfloat16
F32 = jnp.float32
NX, NC, NY, NZ = 4, 2, 4, 8
NE = NY * NZ
MOST = 8
SLOTS = NE * MOST
DZ = (0, 1, 7, 4, 2, 6, 3, 5)
BOUND = (0, 5, 8)
CHUNKS = len(DZ)
PER = NE // CHUNKS
GROUPS = len(BOUND) - 1
STEP = PER * MOST
NT = (((1,), (1,)), ((), ()))
TN = (((0,), (0,)), ((), ()))


A, B = 0, 1
SCHEDULE = tuple(("send", n) for n in range(CHUNKS)) + (
    ("own", 0), ("own", 1), ("own", 2),
    ("near", 0), ("near", 1), ("near", 2), ("own", 3), ("own", 4), ("far", 0), ("far", 1), ("far", 2),
    ("front", A, 0), ("near", 3), ("near", 4), ("front", A, 1), ("own", 5), ("own", 6), ("far", 3), ("far", 4),
    ("front", A, 2), ("front", A, 6), ("own", 7), ("front", A, 3), ("front", A, 7), ("front", A, 4),
    ("front", A, 5), ("middle", A),
    ("out", A, 2), ("mine", A, 2), ("near", 5), ("out", A, 1), ("paired", A, 2), ("near", 6), ("mine", A, 1),
    ("out", A, 3), ("paired", A, 1), ("near", 7), ("mine", A, 3), ("far", 5), ("out", A, 0), ("paired", A, 3),
    ("mine", A, 0), ("far", 6), ("front", B, 0), ("front", B, 1), ("front", B, 2), ("front", B, 6), ("relayed", A),
    ("front", B, 3), ("front", B, 7), ("far", 7), ("front", B, 4), ("front", B, 5), ("middle", B), ("route_parts",),
    ("out", B, 2), ("mine", B, 2), ("out", B, 1), ("paired", B, 2), ("mine", B, 1), ("out", B, 3), ("paired", B, 1),
    ("mine", B, 3), ("paired", A, 0), ("finished", A), ("out", B, 0), ("paired", B, 3), ("mine", B, 0),
    ("route_back",), ("paired", B, 0), ("relayed", B), ("finished", B),
)


def kernel(tok, og, ids, rw, wg_h, wu_h, wd_h, tg_out, rg_out,
           wgu, wd, packed, xg, acc, gbuf, ps, pb, own, relay, snd, fin, rets, ret,
           selbuf, rpart, rtot, rret,
           wsem, disp_r, ag_r, far_r, core_r, pair_r, rel_r, fin_r, ret_r, rp_r, rr_r, send_s):
    seq, exp = lax.axis_index("seq"), lax.axis_index("exp")
    x, c = seq // NC, seq % NC
    y, z = exp // NZ, exp % NZ
    f = tok.shape[1]

    def at_x(step, flip=0):
        return {"seq": NC * ((x + step) % NX) + (c + flip) % NC}

    def to_exp(i, dy):
        return {"exp": ((y + dy) % NY) * NZ + (z + DZ[i]) % NZ}

    def from_exp(i, dy):
        return {"exp": ((y + NY - dy) % NY) * NZ + (z + NZ - DZ[i]) % NZ}

    def copy(src, dst, ssem, rsem, dev):
        return pltpu.make_async_remote_copy(
            src_ref=src, dst_ref=dst, send_sem=ssem, recv_sem=rsem,
            device_id=dev, device_id_type=MESH)

    def got(ref, sem):
        pltpu.make_async_copy(ref, ref, sem).wait()

    barrier = pltpu.get_barrier_semaphore()

    for n in (3, 6, 7, 4, 5, 1, 2, 0):
        @pl.loop(1 if n == 0 else 0, NY)
        def _(dy):
            pl.semaphore_signal(barrier, inc=1, device_id=to_exp(n, dy), device_id_type=MESH)

    for k in range(1, NX * NC):
        pl.semaphore_signal(barrier, inc=1, device_id=at_x(k // NC, k % NC), device_id_type=MESH)

    wcopies = []
    for k in range(NX * NC):
        dx, flip = k // NC, k % NC
        first = pl.multiple_of((NC * ((x + NX - dx) % NX) + (c + flip) % NC) * f, 128)
        h = wg_h.shape[1]
        for n, (src, dst) in enumerate((
                (wg_h.at[pl.ds(first, f), :], wgu.at[k, :, 0:h]),
                (wu_h.at[pl.ds(first, f), :], wgu.at[k, :, h:2 * h]),
                (wd_h.at[:, pl.ds(first, f)], wd.at[k]))):
            one = pltpu.make_async_copy(src, dst, wsem.at[k, n])
            one.start()
            wcopies.append(one)

    q = lax.broadcasted_iota(jnp.int32, (SLOTS, tok.shape[0]), 0)
    j = q >> 3
    i = j >> 2
    dz = jnp.zeros_like(i)
    for n in range(1, CHUNKS):
        dz = jnp.where(i == n, DZ[n], dz)
    wanted = ((y + (j & 3)) & 3) * NZ + ((z + dz) & 7)
    hot = ids[0:1, :] == wanted
    for k in range(1, ids.shape[0]):
        hot = hot | (ids[k:k + 1, :] == wanted)
    hot = jnp.where(hot, 1.0, 0.0)
    t0 = lax.broadcasted_iota(jnp.int32, (tok.shape[0], tok.shape[0]), 0)
    t1 = lax.broadcasted_iota(jnp.int32, (tok.shape[0], tok.shape[0]), 1)
    before = jnp.where(t0 < t1, 1.0, 0.0).astype(BF)
    rank = jnp.dot(hot.astype(BF), before, preferred_element_type=F32)
    sel = jnp.where(rank == (q & 7).astype(F32), hot, 0.0)
    selbuf[...] = sel
    selb = sel.astype(BF)
    for n, src in enumerate((tok, og)):
        rows = jnp.dot(selb, src[...], preferred_element_type=F32)
        rows = rows.reshape(NE, MOST, f).astype(BF)
        packed[:, :, n * f:(n + 1) * f] = rows
        xg[0, 0:1, :, n * f:(n + 1) * f] = rows[0:1]

    pl.semaphore_wait(barrier, NE - 1 + NX * NC - 1)

    def send(n):
        @pl.loop(1 if n == 0 else 0, NY)
        def _(dy):
            j = n * PER + dy
            copy(packed.at[j], xg.at[0, j], send_s.at[0], disp_r.at[n], to_exp(n, dy)).start()

    def group_of(r):
        return sum(r >= b for b in BOUND[1:-1])

    def group(g):
        return slice(BOUND[g] * STEP, BOUND[g + 1] * STEP)

    def size(g):
        return (BOUND[g + 1] - BOUND[g]) * STEP

    def rows_of(r):
        return pl.ds(r * PER, PER)

    def own_chunk(r):
        lo = 1 if r == 0 else r * PER
        got(xg.at[0, lo:(r + 1) * PER], disp_r.at[r])
        mine = xg.at[0, rows_of(r)]
        copy(mine, xg.at[2, rows_of(r)], send_s.at[1], ag_r.at[0, r], at_x(1)).start()
        copy(mine, xg.at[6, rows_of(r)], send_s.at[2], ag_r.at[1, r], at_x(3)).start()
        copy(mine, xg.at[1, rows_of(r)], send_s.at[3], core_r.at[0, group_of(r)], at_x(0, 1)).start()

    hp = PER // 2

    def near_chunk(r):
        for n, (slot, step) in enumerate(((2, 1), (6, 3))):
            part = xg.at[slot, rows_of(r)]
            got(part, ag_r.at[n, r])
            lo = r * PER + n * hp
            copy(xg.at[slot, lo:lo + hp], xg.at[4, lo:lo + hp], send_s.at[4 + n], far_r.at[n, r], at_x(step)).start()
            copy(part, xg.at[slot + 1, rows_of(r)], send_s.at[6 + n], core_r.at[slot // 2, group_of(r)], at_x(0, 1)).start()

    def far_chunk(r):
        for n in range(2):
            lo = r * PER + n * hp
            got(xg.at[4, lo:lo + hp], far_r.at[n, r])
        copy(xg.at[4, rows_of(r)], xg.at[5, rows_of(r)], send_s.at[8], core_r.at[2, group_of(r)], at_x(0, 1)).start()

    h2 = wgu.shape[2]

    def front(g, k):
        for n in range(3):
            if wcopies[3 * k + n] is not None:
                wcopies[3 * k + n].wait()
                wcopies[3 * k + n] = None
        blocks = slice(BOUND[g] * PER, BOUND[g + 1] * PER)
        rows = group(g)
        if k % 2:
            got(xg.at[k, blocks], core_r.at[k // 2, g])
        xs = xg[k, blocks, :, 0:f].reshape(size(g), f)
        ds = xg[k, blocks, :, f:2 * f].reshape(size(g), f)
        gu = jnp.dot(xs, wgu[k], preferred_element_type=F32)
        bg = lax.dot_general(ds, wd[k], NT, preferred_element_type=F32)
        if k == 0:
            acc[rows, 0:h2] = gu
            acc[rows, h2:] = bg
        else:
            acc[rows, 0:h2] += gu
            acc[rows, h2:] += bg

    h = h2 // 2

    def middle(g):
        rows = group(g)
        pre_g = acc[rows, 0:h]
        pre_u = acc[rows, h:h2]
        back = acc[rows, h2:]
        sig = 1.0 / (1.0 + jnp.exp(-pre_g))
        active = pre_g * sig
        gbuf[rows, 0:h] = (back * pre_u * sig * (1.0 + pre_g * (1.0 - sig))).astype(BF)
        gbuf[rows, h:h2] = (back * active).astype(BF)
        part = lax.dot_general(jnp.ones((8, h), F32), active * pre_u * back, NT, preferred_element_type=F32,
                               precision=lax.Precision.HIGHEST)
        rpart[0, :, rows] = part[0:1, :]

    def product(g, d, flip):
        k = ((NX - d) % NX) * NC + flip
        return lax.dot_general(gbuf[group(g)], wgu[k], NT, preferred_element_type=F32)

    def half(g, n):
        first, m = BOUND[g] * STEP, size(g) // 2
        return slice(first + n * m, first + (n + 1) * m)

    def passing(g):
        return slice(BOUND[g] * STEP // 2, BOUND[g + 1] * STEP // 2)

    def out(g, d):
        rows = group(g)
        ps[d, rows] = product(g, d, 1).astype(BF)
        copy(ps.at[d, rows], pb.at[d, rows], send_s.at[10], pair_r.at[d, g], at_x(0, 1)).start()

    def mine(g, d):
        own[d, group(g)] = product(g, d, 0)

    def paired(g, d):
        rows = group(g)
        got(pb.at[d, rows], pair_r.at[d, g])
        if d == 0:
            own[0, rows] += pb[0, rows].astype(F32)
        elif d == 2:
            snd[0, rows] = (own[2, rows] + pb[2, rows].astype(F32)).astype(BF)
            for n, step in enumerate((1, 3)):
                copy(snd.at[0, half(g, n)], relay.at[n, passing(g)], send_s.at[11 + n], rel_r.at[n, g], at_x(step)).start()
        else:
            n = 0 if d == 1 else 1
            own[d, rows] += pb[d, rows].astype(F32)
            other = half(g, 1 - n)
            snd[1 + n, other] = own[d, other].astype(BF)
            copy(snd.at[1 + n, other], fin.at[n, other], send_s.at[13 + n], fin_r.at[n, 1 - n, g], at_x(d)).start()

    def relayed(g):
        for n, d in enumerate((1, 3)):
            got(relay.at[n, passing(g)], rel_r.at[n, g])
            this = half(g, n)
            snd[1 + n, this] = (own[d, this] + relay[n, passing(g)].astype(F32)).astype(BF)
            copy(snd.at[1 + n, this], fin.at[n, this], send_s.at[15 + n], fin_r.at[n, n, g], at_x(d)).start()

    def finished(g):
        for n in (1, 0):
            this = half(g, n)
            got(fin.at[0, this], fin_r.at[0, n, g])
            got(fin.at[1, this], fin_r.at[1, n, g])
            s = own[0, this] + fin[0, this].astype(F32) + fin[1, this].astype(F32)
            lo, hi = this.start // MOST, this.stop // MOST
            s = s.reshape(hi - lo, MOST, f).astype(BF)
            rets[lo:hi] = s
            if lo == 0:
                ret[0:1] = s[0:1]
            for r in range(CHUNKS):
                first, last = max(lo, r * PER, 1) - r * PER, min(hi, (r + 1) * PER) - r * PER
                if first >= last:
                    continue

                @pl.loop(first, last)
                def _(dy):
                    j = r * PER + dy
                    copy(rets.at[j], ret.at[j], send_s.at[18], ret_r, from_exp(r, dy)).start()

    def route_parts():
        for k in range(1, NX * NC):
            copy(rpart.at[0], rpart.at[k], send_s.at[9], rp_r, at_x(k // NC, k % NC)).start()

    def route_back():
        got(rpart.at[1:8], rp_r)
        total = rpart[0]
        for k in range(1, NX * NC):
            total = total + rpart[k]
        rtot[...] = total
        rret[0] = total
        for r in range(CHUNKS):
            @pl.loop(1 if r == 0 else 0, NY)
            def _(dy):
                copy(rtot, rret.at[r * PER + dy], send_s.at[17], rr_r, from_exp(r, dy)).start()

    step_of = {"own": own_chunk, "near": near_chunk, "far": far_chunk, "front": front, "middle": middle,
               "out": out, "mine": mine, "send": send, "paired": paired, "relayed": relayed, "finished": finished,
               "route_parts": route_parts, "route_back": route_back}
    for step in SCHEDULE:
        step_of[step[0]](*step[1:])

    got(rret.at[1:NE], rr_r)
    lane = lax.broadcasted_iota(jnp.int32, (NE, 1, SLOTS), 2) >> 3
    row = lax.broadcasted_iota(jnp.int32, (NE, 1, SLOTS), 0)
    by_slot = jnp.sum(jnp.where(lane == row, rret[...], 0.0), axis=0)
    by_token = jnp.dot(jnp.broadcast_to(by_slot, (8, SLOTS)), selbuf[...], preferred_element_type=F32,
                       precision=lax.Precision.HIGHEST)
    rg_out[...] = jnp.where(ids[pl.ds(seq, 1), :] < NE, by_token[0:1, :], 0.0)

    weight = jnp.sum(jnp.where(ids[...] < NE, rw[...], 0.0), axis=0, keepdims=True)
    scale = jnp.sum(selbuf[...] * weight, axis=1, keepdims=True)
    got(ret.at[1:NE], ret_r)
    rows = (ret[...].reshape(SLOTS, f).astype(F32) * scale).astype(BF)
    tg_out[...] = lax.dot_general(selbuf[...].astype(BF), rows, TN, preferred_element_type=F32).astype(BF)

    got(packed.at[1:NE], send_s.at[0])
    for n in range(1, 4):
        got(xg.at[0], send_s.at[n])
    for n in range(2):
        got(xg.at[0, 0:NE // 2], send_s.at[4 + n])
        got(xg.at[0], send_s.at[6 + n])
    got(xg.at[0], send_s.at[8])
    got(rpart.at[1:8], send_s.at[9])
    got(ps, send_s.at[10])
    for n in range(11, 17):
        got(relay.at[0], send_s.at[n])
    got(rret.at[1:NE], send_s.at[17])
    got(rets.at[1:NE], send_s.at[18])


def local(tokens, out_grad, expert_ids, route_weights, gate_proj, up_proj, down_proj):
    t, f = tokens.shape
    h = gate_proj.shape[2]
    vmem = pl.BlockSpec(memory_space=pltpu.VMEM)
    anym = pl.BlockSpec(memory_space=pl.ANY)
    dma = pltpu.SemaphoreType.DMA
    token_grad, route_grad = pl.pallas_call(
        kernel,
        out_shape=(jax.ShapeDtypeStruct((t, f), BF), jax.ShapeDtypeStruct((1, t), F32)),
        in_specs=[vmem] * 4 + [anym] * 3,
        out_specs=(vmem, vmem),
        scratch_shapes=[
            pltpu.VMEM((8, f, 2 * h), BF),
            pltpu.VMEM((8, h, f), BF),
            pltpu.VMEM((NE, MOST, 2 * f), BF),
            pltpu.VMEM((8, NE, MOST, 2 * f), BF),
            pltpu.VMEM((SLOTS, 3 * h), F32),
            pltpu.VMEM((SLOTS, 2 * h), BF),
            pltpu.VMEM((4, SLOTS, f), BF),
            pltpu.VMEM((4, SLOTS, f), BF),
            pltpu.VMEM((4, SLOTS, f), F32),
            pltpu.VMEM((2, SLOTS // 2, f), BF),
            pltpu.VMEM((3, SLOTS, f), BF),
            pltpu.VMEM((2, SLOTS, f), BF),
            pltpu.VMEM((NE, MOST, f), BF),
            pltpu.VMEM((NE, MOST, f), BF),
            pltpu.VMEM((SLOTS, t), F32),
            pltpu.VMEM((8, 1, SLOTS), F32),
            pltpu.VMEM((1, SLOTS), F32),
            pltpu.VMEM((NE, 1, SLOTS), F32),
            dma((8, 3)), dma((CHUNKS,)), dma((2, CHUNKS)), dma((2, CHUNKS)), dma((4, GROUPS)),
            dma((4, GROUPS)), dma((2, GROUPS)), dma((2, 2, GROUPS)), dma(()), dma(()), dma(()), dma((19,)),
        ],
        compiler_params=pltpu.CompilerParams(
            collective_id=0, has_side_effects=True, vmem_limit_bytes=60 * 1024 * 1024),
        name="moe_back",
    )(tokens, out_grad, expert_ids.T, route_weights.T, gate_proj[0], up_proj[0], down_proj[0])
    return token_grad, route_grad.reshape(t, 1)


def solution(mesh):
    in_specs = (
        P("exp", "seq"),
        P("exp", "seq"),
        P("exp", None),
        P("exp", None),
        P("exp", None, "seq"),
        P("exp", None, "seq"),
        P("exp", "seq", None),
    )
    out_specs = (P("exp", "seq"), P("exp", "seq"))
    return jax.shard_map(local, mesh=mesh, in_specs=in_specs, out_specs=out_specs, check_vma=False)
```
